512 devices in a mesh: leaf: 8 (over y), grow: 8 (over z), gcol: 8 (over x, core).
Axes of the slice: x: 4, y: 8, z: 8, core: 2. Of those that a mesh axis runs over, the one named last changes fastest.
Arguments:
- right_leaf: float32 [8, 8, 8, 512, 256], P('leaf', 'grow', 'gcol'), may hold values from -6 to 6
- inverse_leaf: float32 [8, 8, 8, 512, 512], P('leaf', 'grow', 'gcol'), may hold values from -2 to 2
- lower_leaf: float32 [8, 8, 8, 512, 512], P('leaf', 'grow', 'gcol'), may hold values from -0.25 to 0.25
- present: int32 [8, 8, 8], P('leaf', 'grow', 'gcol'), may hold values 0 or 1
- right_middle: float32 [8, 8, 512, 256], P('leaf', 'grow', 'gcol'), may hold values from -6 to 6
- inverse_middle: float32 [8, 8, 512, 512], P('leaf', 'grow', 'gcol'), may hold values from -2 to 2
- upper_middle: float32 [2, 8, 8, 512, 512], P(None, 'leaf', 'grow', 'gcol'), may hold values from -0.03125 to 0.03125
- right_top: float32 [2, 512, 256], P(None, 'gcol'), may hold values from -6 to 6
- inverse_top: float32 [2, 512, 512], P(None, 'gcol'), may hold values from -2 to 2
- upper_top: float32 [1, 512, 512], P(None, 'gcol'), may hold values from -0.25 to 0.25
Outputs:
- solve_leaf: float32 [8, 8, 8, 512, 256], P('leaf', 'grow', 'gcol')
- solve_middle: float32 [8, 8, 512, 256], P('leaf', 'grow', 'gcol')
- solve_top: float32 [2, 512, 256], P(None, 'gcol')
The draws below stay inside these ranges and needn't reach their ends.
All inputs are finite; a program needn't handle non-finite values. No bound on the sum of `present` on one device may be relied on, other than what follows from the above.
Results may differ from the reference program's by a relative error of at most 0.00016.
Values sent between devices are 32-bit elements; how exact they have to be, the bound alone decides.
No kernel may reach another device: no remote copies, remote signals or barrier semaphores. Data moves between devices by JAX's collectives and lax.ppermute only.
A program may use at most 64 MiB of HBM per device.

```python
import math
import jax
import jax.numpy as jnp
from jax import lax

BLK = 512
NRHS = 256
LEVELS = 2
LAYERS = 8
PROW = 8
PCOL = 8
PAIRS = 1


def dominant(key, shape):
    noise_key = jax.random.fold_in(key, 11)
    scale_key = jax.random.fold_in(key, 12)
    noise = jax.random.normal(noise_key, shape, jnp.float32) * (0.6 / math.sqrt(BLK))
    scales = jax.random.uniform(scale_key, shape[:-1] + (1,), jnp.float32, 0.7, 1.4)
    identity = jnp.eye(BLK, dtype=jnp.float32)
    return jnp.clip(identity * scales + noise, -2.0, 2.0)


def draw_inverse_leaf(key, part):
    return dominant(key, (LAYERS, PROW, PCOL, BLK, BLK))


def draw_inverse_middle(key, part):
    return dominant(key, (LAYERS, PROW, BLK, BLK))


def draw_inverse_top(key, part):
    return dominant(key, (LEVELS, BLK, BLK))


def plant(values, rng, low, top_value):
    extent = values.shape
    index_at = [jax.random.randint(jax.random.fold_in(rng, axis), (), 0, extent[axis]) for axis in range(len(extent))]
    values = values.at[tuple(index_at)].set(low)
    longest = extent.index(max(extent))
    index_at[longest] = (index_at[longest] + 1) % extent[longest]
    return values.at[tuple(index_at)].set(top_value)


def block_levels(own_key, shape, pieces, smallest, high):
    gain = 1.0
    for dim, blocks in pieces:
        steps = jax.random.uniform(jax.random.fold_in(jax.random.fold_in(own_key, 6), dim), (blocks,), jnp.float32, smallest / len(pieces), high / len(pieces))
        gain = gain * jnp.repeat(jnp.exp(steps), shape[dim] // blocks).reshape((-1,) + (1,) * (len(shape) - 1 - dim))
    return gain


def bell_draw(own_key, dims, width, bound, shards=(), kind=jnp.bfloat16):
    values = width * jax.random.normal(own_key, dims, jnp.float32)
    if shards:
        values = values * block_levels(own_key, dims, shards, -0.22, 0.18)
    return jnp.clip(values, -bound, bound).astype(kind)


def setup_inputs(seed: int = 0) -> dict:
    arg_keys = jax.random.split(jax.random.key(seed), 11)
    return {
        "right_leaf": bell_draw(arg_keys[0], (LAYERS, PROW, PCOL, BLK, NRHS), 1.0, 6.0, ((0, 8), (1, 8), (2, 8)), jnp.float32),
        "inverse_leaf": draw_inverse_leaf(jax.random.fold_in(arg_keys[10], 71), 0),
        "lower_leaf": bell_draw(arg_keys[2], (LAYERS, PROW, PCOL, BLK, BLK), BLK ** -0.5, 0.25, ((0, 8), (1, 8), (2, 8)), jnp.float32),
        "present": plant((jax.random.randint(arg_keys[3], (LAYERS, PROW, PCOL), 0, 4) < 3).astype(jnp.int32), jax.random.fold_in(arg_keys[3], 1), 0, 1),
        "right_middle": bell_draw(arg_keys[4], (LAYERS, PROW, BLK, NRHS), 1.0, 6.0, ((0, 8), (1, 8), (2, 8)), jnp.float32),
        "inverse_middle": draw_inverse_middle(jax.random.fold_in(arg_keys[10], 71), 0),
        "upper_middle": bell_draw(arg_keys[6], (LEVELS, LAYERS, PROW, BLK, BLK), (BLK * LAYERS * PROW) ** -0.5, 0.03125, ((1, 8), (2, 8), (3, 8)), jnp.float32),
        "right_top": bell_draw(arg_keys[7], (LEVELS, BLK, NRHS), 1.0, 6.0, ((1, 8),), jnp.float32),
        "inverse_top": draw_inverse_top(jax.random.fold_in(arg_keys[10], 71), 0),
        "upper_top": bell_draw(arg_keys[9], (PAIRS, BLK, BLK), BLK ** -0.5, 0.25, ((1, 8),), jnp.float32),
    }


PRECISE = lax.Precision.HIGHEST


def product(formula, first_arg, second_arg):
    return jnp.einsum(formula, first_arg, second_arg, precision=PRECISE, preferred_element_type=jnp.float32)


def pair_index(upper_level, lower_level):
    return upper_level * (upper_level - 1) // 2 + lower_level


def reference(right_leaf, inverse_leaf, lower_leaf, present, right_middle, inverse_middle, upper_middle, right_top, inverse_top, upper_top):
    present_scale = present.astype(jnp.float32)[..., None, None]
    leaf_fwd = product('lrcij,lrcjn->lrcin', inverse_leaf, right_leaf)
    middle_sum = product('lrcij,lrcjn->lrin', lower_leaf, leaf_fwd * present_scale)
    middle_fwd = product('lrij,lrjn->lrin', inverse_middle, right_middle - middle_sum)
    top_sum = product('klrji,lrjn->kin', upper_middle, middle_fwd)
    top_fwd = []
    for upper_level in range(LEVELS):
        residual = right_top[upper_level] - top_sum[upper_level]
        for lower_level in range(upper_level):
            residual = residual - product('ji,jn->in', upper_top[pair_index(upper_level, lower_level)], top_fwd[lower_level])
        top_fwd.append(product('ij,jn->in', inverse_top[upper_level], residual))
    top_back = [None] * LEVELS
    for upper_level in reversed(range(LEVELS)):
        residual = top_fwd[upper_level]
        for higher_level in range(upper_level + 1, LEVELS):
            residual = residual - product('ij,jn->in', upper_top[pair_index(higher_level, upper_level)], top_back[higher_level])
        top_back[upper_level] = product('ji,jn->in', inverse_top[upper_level], residual)
    solve_top = jnp.stack(top_back)
    middle_res = middle_fwd - product('klrij,kjn->lrin', upper_middle, solve_top)
    solve_middle = product('lrji,lrjn->lrin', inverse_middle, middle_res)
    leaf_res = leaf_fwd - product('lrcji,lrjn->lrcin', lower_leaf, solve_middle) * present_scale
    solve_leaf = product('lrcji,lrcjn->lrcin', inverse_leaf, leaf_res)
    return solve_leaf, solve_middle, solve_top
```

```python
import jax
import jax.numpy as jnp
from jax import lax
from jax.sharding import Mesh
from jax.sharding import PartitionSpec as P

GX, GC = "gcol_0", "gcol_1"
GCOL = (GX, GC)
LG = ("leaf", "grow")
PRECISE = lax.Precision.HIGHEST


def dot(a, b, ca, cb):
    return lax.dot_general(
        a, b, (((ca,), (cb,)), ((), ())), precision=PRECISE, preferred_element_type=jnp.float32
    )


def swap(x, axis):
    return lax.all_to_all(x, axis, split_axis=0, concat_axis=0, tiled=True)


def shift(x, axis, step):
    n = lax.axis_size(axis)
    return lax.ppermute(x, axis, [(s, (s + step) % n) for s in range(n)])


def spread(x, n):
    return jnp.broadcast_to(x[None], (n, *x.shape))


def split_rows(blocks, parts, rows):
    stacked = jnp.concatenate(blocks, axis=0).reshape(-1, parts, rows, blocks[0].shape[-1])
    return [stacked[:, i].reshape(-1, blocks[0].shape[-1]) for i in range(parts)]


def local(
    right_leaf,
    inverse_leaf,
    lower_leaf,
    present,
    right_middle,
    inverse_middle,
    upper_middle,
    right_top,
    inverse_top,
    upper_top,
):
    n_x, n_lg = lax.axis_size(GX), lax.axis_size(LG)
    n_g = n_x * lax.axis_size(GC)
    block, nrhs = right_leaf.shape[-2:]
    share = block // n_g
    cols = nrhs // n_g
    me = lax.axis_index(GCOL)
    il, ll, rl = inverse_leaf[0, 0, 0], lower_leaf[0, 0, 0], right_leaf[0, 0, 0]
    kept = present[0, 0, 0].astype(jnp.float32)

    with jax.named_scope("gather_w"):
        w = jnp.concatenate([inverse_middle[0, 0], upper_middle[0, 0, 0], upper_middle[1, 0, 0]], axis=0)
        w_mine = swap(spread(w, n_x), GX).reshape(-1, block)
    with jax.named_scope("gather_t"):
        t = jnp.concatenate([inverse_top[0], inverse_top[1], upper_top[0]], axis=0)
    with jax.named_scope("leaf_fwd"):
        leaf_fwd = dot(il, rl, 1, 0)
        part = dot(leaf_fwd, ll, 0, 1) * kept
        lane = lax.broadcasted_iota(jnp.int32, (1, block), 1)
        own = (lane >= me * share) & (lane < (me + 1) * share)
        rm = right_middle[0, 0].T
        part = jnp.where(own, jnp.concatenate([rm] * n_g, axis=1), 0.0) - part
        sent = jnp.concatenate([part, right_top[0].T, right_top[1].T], axis=1)
        sent = sent.reshape(n_g, cols, -1)
    with jax.named_scope("core_w"):
        w_other = shift(w_mine, GC, 1)
    with jax.named_scope("leaf_swap"):
        got = swap(sent, GCOL)
    with jax.named_scope("mid_fwd"):
        rhs = jnp.sum(got[:, :, :block], axis=0)
        rt = [
            jnp.concatenate([got[c, :, block + k * share : block + (k + 1) * share] for c in range(n_g)], axis=1)
            for k in range(2)
        ]
        im, um0, um1 = split_rows([w_mine, w_other], 3, share)
        mf = dot(rhs, im, 1, 1)
        tp = jnp.concatenate([dot(mf, um0, 1, 0), dot(mf, um1, 1, 0)], axis=1)
        pieces = tp.reshape(cols, -1, 128).swapaxes(0, 1).reshape(n_lg, -1, 128)
    with jax.named_scope("gather_t"):
        ts = [t, shift(t, GX, 1), shift(t, GX, -1), shift(t, GX, 2)]
        t_mine = jnp.concatenate(ts, axis=0)
    with jax.named_scope("top_scatter"):
        pieces = swap(pieces, LG)
        total = spread(jnp.sum(pieces, axis=0), n_lg)
    with jax.named_scope("core_t"):
        t_other = shift(t_mine, GC, 1)
        it0, it1, ut = split_rows([t_mine, t_other], 3, share)
    with jax.named_scope("top_gather"):
        total = swap(total, LG)
        total = total.reshape(-1, cols, 128).swapaxes(0, 1).reshape(cols, -1)
    with jax.named_scope("top_solve"):
        f0 = dot(rt[0] - total[:, :block], it0, 1, 1)
        f1 = dot(rt[1] - total[:, block:] - dot(f0, ut, 1, 0), it1, 1, 1)
        s1 = dot(f1, it1, 1, 0)
        s0 = dot(f0 - dot(s1, ut, 1, 1), it0, 1, 0)
    with jax.named_scope("mid_bwd"):
        mr = mf - dot(s0, um0, 1, 1) - dot(s1, um1, 1, 1)
        sm = dot(mr, im, 1, 0)
        s0 = s0.reshape(cols, n_g, share).swapaxes(0, 1)
        s1 = s1.reshape(cols, n_g, share).swapaxes(0, 1)
        back = jnp.concatenate([spread(sm, n_g), s0, s1], axis=2)
    with jax.named_scope("back_swap"):
        back = swap(back, GCOL)
    with jax.named_scope("leaf_bwd"):
        back = back.reshape(nrhs, -1)
        sm = back[:, :block]
        leaf_res = leaf_fwd - dot(ll, sm, 0, 1) * kept
        leaf_back = dot(il, leaf_res, 0, 0)
        solve_middle = lax.dynamic_slice_in_dim(sm, me * share, share, 1).T
        solve_top = jnp.stack([back[:, block + k * share : block + (k + 1) * share].T for k in range(2)])
    return (leaf_back[None, None, None], solve_middle[None, None], solve_top)


def solution(mesh):
    split = Mesh(
        mesh.devices.reshape(mesh.shape["leaf"], mesh.shape["grow"], mesh.shape["gcol"] // 2, 2),
        ("leaf", "grow", GX, GC),
    )
    in_specs = (
        P("leaf", "grow", GCOL, None, None),
        P("leaf", "grow", GCOL, None, None),
        P("leaf", "grow", GCOL, None, None),
        P("leaf", "grow", GCOL),
        P("leaf", "grow", GCOL, None),
        P("leaf", "grow", GCOL, None),
        P(None, "leaf", "grow", GCOL, None),
        P(None, GCOL, None),
        P(None, GCOL, None),
        P(None, GCOL, None),
    )
    out_specs = (
        P("leaf", "grow", GCOL, None, None),
        P("leaf", "grow", GCOL, None),
        P(None, GCOL, None),
    )
    return jax.shard_map(local, mesh=split, in_specs=in_specs, out_specs=out_specs, check_vma=False)
```

```python
import jax
import jax.numpy as jnp
from jax import lax
from jax.experimental import pallas as pl
from jax.experimental.pallas import tpu as pltpu
from jax.sharding import Mesh
from jax.sharding import PartitionSpec as P

GX, GC = "gcol_0", "gcol_1"
GCOL = (GX, GC)
LG = ("leaf", "grow")
PRECISE = lax.Precision.HIGHEST


def dot(a, b, ca, cb):
    return lax.dot_general(
        a, b, (((ca,), (cb,)), ((), ())), precision=PRECISE, preferred_element_type=jnp.float32
    )


def swap(x, axis):
    return lax.all_to_all(x, axis, split_axis=0, concat_axis=0, tiled=True)


def shift(x, axis, step):
    n = lax.axis_size(axis)
    return lax.ppermute(x, axis, [(s, (s + step) % n) for s in range(n)])


def f32(*shape):
    return jax.ShapeDtypeStruct(shape, jnp.float32)


def kernel_call(body, outs, *args, scalars=0, scratch=(), limit=24):
    specs = [pl.BlockSpec(memory_space=pltpu.SMEM)] * scalars
    specs += [pl.BlockSpec(memory_space=pltpu.VMEM)] * (len(args) - scalars)
    out_specs = jax.tree.map(lambda _: pl.BlockSpec(memory_space=pltpu.VMEM), outs)
    return pl.pallas_call(
        body, out_shape=outs, in_specs=specs, out_specs=out_specs, scratch_shapes=scratch,
        compiler_params=pltpu.CompilerParams(vmem_limit_bytes=limit << 20),
    )(*args)


def split(x):
    high = x.astype(jnp.bfloat16)
    return high, (x - high.astype(jnp.float32)).astype(jnp.bfloat16)


def dot3(a, b, ca, cb):
    def one(x, y):
        return lax.dot_general(
            x, y, (((ca,), (cb,)), ((), ())), preferred_element_type=jnp.float32
        )

    (ah, al), (bh, bl) = a, b
    return one(ah, bh) + (one(ah, bl) + one(al, bh))


def pack_kernel(im, um, it, ut, w, t, sems):
    share = im.shape[0]
    copies = [
        pltpu.make_async_copy(src, out.at[pl.ds(at * share, src.shape[0])], sems.at[i])
        for i, (src, out, at) in enumerate([(im, w, 0), (um, w, 1), (it, t, 0), (ut, t, 2)])
    ]
    for c in copies:
        c.start()
    for c in copies:
        c.wait()


def fill(high, low, blocks, part, share):
    n = 0
    for ref in blocks:
        for s in range(ref.shape[0] // (3 * share)):
            at = (3 * s + part) * share
            h, l = split(ref[at : at + share])
            high[n * share : (n + 1) * share] = h
            low[n * share : (n + 1) * share] = l
            n += 1
    return high[...], low[...]


def mid_kernel(got, mine, other, pieces, mf_out, high, low):
    blocks = [mine, other]
    n_x, cols, _ = got.shape
    block = other.shape[1]
    share = mine.shape[0] // (3 * n_x)
    rhs = got[0, :, :block]
    for c in range(1, n_x):
        rhs = rhs + got[c, :, :block]
    mf = dot3(split(rhs), fill(high.at[0], low.at[0], blocks, 0, share), 1, 1)
    mf_out[...] = mf
    mfs = split(mf)
    rows = pieces.shape[1]
    per = cols // rows
    for k in range(2):
        tp = dot3(mfs, fill(high.at[1 + k], low.at[1 + k], blocks, 1 + k, share), 1, 0)
        for j in range(block // 128):
            for i in range(per):
                at = (k * (block // 128) + j) * per + i
                pieces[at] = tp[i * rows : (i + 1) * rows, j * 128 : (j + 1) * 128]


def sum_kernel(pieces, out):
    total = jnp.sum(pieces[...], axis=0)
    out[...] = jnp.broadcast_to(total[None], out.shape)


def top_kernel(got, total, mf, t_mine, t_other, mine, other, back, r, high, low, w_high, w_low):
    n_x, cols, _ = got.shape
    n_g, block = back.shape[0], other.shape[1]
    share = block // n_g
    two = 2 * share
    rows = total.shape[1]
    per = cols // rows
    for j in range(2 * block // 128):
        for i in range(per):
            r[i * rows : (i + 1) * rows, j * 128 : (j + 1) * 128] = total[j * per + i]
    for k in range(2):
        for x in range(n_x):
            at = k * block + x * two
            r[:, at : at + two] = got[x, :, block + k * two : block + (k + 1) * two] - r[:, at : at + two]
    it0, it1, ut = (
        fill(high.at[p], low.at[p], [t_mine, t_other], p, share) for p in range(3)
    )
    f0 = dot3(split(r[:, :block]), it0, 1, 1)
    f1 = dot3(split(r[:, block:] - dot3(split(f0), ut, 1, 0)), it1, 1, 1)
    s1 = dot3(split(f1), it1, 1, 0)
    s1s = split(s1)
    s0 = dot3(split(f0 - dot3(s1s, ut, 1, 1)), it0, 1, 0)
    im, um0, um1 = (fill(w_high.at[p], w_low.at[p], [mine, other], p, share) for p in range(3))
    mr = mf[...] - dot3(split(s0), um0, 1, 1) - dot3(s1s, um1, 1, 1)
    sm = dot3(split(mr), im, 1, 0)
    for d in range(n_g):
        back[d, :, :block] = sm
        back[d, :, block : block + share] = s0[:, d * share : (d + 1) * share]
        back[d, :, block + share :] = s1[:, d * share : (d + 1) * share]


def end_kernel(me, back, link, lead, leaf_out, mid_out, top_out):
    n_g, cols, _ = back.shape
    block = link.shape[0]
    share = block // n_g
    both = back[...].reshape(n_g * cols, back.shape[2])
    sm = both[:, :block]
    leaf_out[...] = lead[...] - dot3(split(link[...]), split(sm), 1, 1)
    mine = jnp.zeros((n_g * cols, share), jnp.float32)
    for c in range(n_g):
        mine = jnp.where(me[0] == c, sm[:, c * share : (c + 1) * share], mine)
    mid_out[...] = mine.T
    for k in range(2):
        top_out[k] = both[:, block + k * share : block + (k + 1) * share].T


def local(
    right_leaf,
    inverse_leaf,
    lower_leaf,
    present,
    right_middle,
    inverse_middle,
    upper_middle,
    right_top,
    inverse_top,
    upper_top,
):
    n_x, n_c, n_lg = lax.axis_size(GX), lax.axis_size(GC), lax.axis_size(LG)
    n_g = n_x * n_c
    block, nrhs = right_leaf.shape[-2:]
    share = block // n_g
    cols = nrhs // n_g
    me, core = lax.axis_index(GCOL), lax.axis_index(GC)
    il, ll, rl = inverse_leaf[0, 0, 0], lower_leaf[0, 0, 0], right_leaf[0, 0, 0]
    kept = present[0, 0, 0].astype(jnp.float32)

    any_spec = pl.BlockSpec(memory_space=pl.ANY)
    vmem_spec = pl.BlockSpec(memory_space=pltpu.VMEM)
    w, t = pl.pallas_call(
        pack_kernel,
        out_shape=(f32(3 * share, block), f32(3 * share, block)),
        in_specs=[any_spec] * 4,
        out_specs=(vmem_spec, vmem_spec),
        scratch_shapes=[pltpu.SemaphoreType.DMA((4,))],
        name="pack",
    )(inverse_middle[0, 0], upper_middle.reshape(2 * share, block), inverse_top.reshape(2 * share, block), upper_top[0])
    ws = [w, shift(w, GX, 1), shift(w, GX, -1), shift(w, GX, 2)]
    leaf_fwd = dot(il, rl, 1, 0)
    part = dot(leaf_fwd, ll, 0, 1) * kept
    lane = lax.broadcasted_iota(jnp.int32, (1, block), 1)
    own = (lane >= me * share) & (lane < (me + 1) * share)
    rm = right_middle[0, 0].T
    part = jnp.where(own, jnp.concatenate([rm] * n_g, axis=1), 0.0) - part
    first = lax.broadcasted_iota(jnp.int32, (1, n_c * share), 1) // share == core
    rts = [jnp.where(first, jnp.concatenate([right_top[k].T] * n_c, axis=1), 0.0) for k in range(2)]
    sent = jnp.concatenate([part, *rts], axis=1).reshape(n_x, n_c, cols, -1)
    keep = lax.dynamic_index_in_dim(sent, core, 1, keepdims=False)
    give = lax.dynamic_index_in_dim(sent, 1 - core, 1, keepdims=False)
    take = shift(give, GC, 1)
    keep = keep + take
    lead = dot(il, leaf_fwd, 0, 0)
    link = dot(il, ll, 0, 1) * kept
    got = swap(keep, GX)
    mine = jnp.concatenate(ws, axis=0)
    other = shift(mine, GC, 1)
    ts = [t, shift(t, GX, 1), shift(t, GX, -1), shift(t, GX, 2)]
    halves = pltpu.VMEM((3, block, block), jnp.bfloat16)
    pieces, mf = kernel_call(
        mid_kernel,
        (f32(n_lg, 2 * cols * block // 128 // n_lg, 128), f32(cols, block)),
        got, mine, other, scratch=[halves, halves],
    )
    arrived = swap(pieces, LG)
    t_mine, arrived = lax.optimization_barrier((jnp.concatenate(ts, axis=0), arrived))
    t_other = shift(t_mine, GC, 1)
    total = kernel_call(sum_kernel, pieces, arrived)
    total = swap(total, LG)
    back = kernel_call(
        top_kernel, f32(n_g, cols, block + 2 * share), got, total, mf, t_mine, t_other, mine, other,
        scratch=[pltpu.VMEM((cols, 2 * block), jnp.float32), halves, halves, halves, halves],
    )
    back = swap(back, GCOL)
    leaf_back, solve_middle, solve_top = kernel_call(
        end_kernel,
        (f32(block, nrhs), f32(share, nrhs), f32(2, share, nrhs)),
        me.reshape(1).astype(jnp.int32), back, link, lead, scalars=1,
    )
    return (leaf_back[None, None, None], solve_middle[None, None], solve_top)


def solution(mesh):
    split = Mesh(
        mesh.devices.reshape(mesh.shape["leaf"], mesh.shape["grow"], mesh.shape["gcol"] // 2, 2),
        ("leaf", "grow", GX, GC),
    )
    in_specs = (
        P("leaf", "grow", GCOL, None, None),
        P("leaf", "grow", GCOL, None, None),
        P("leaf", "grow", GCOL, None, None),
        P("leaf", "grow", GCOL),
        P("leaf", "grow", GCOL, None),
        P("leaf", "grow", GCOL, None),
        P(None, "leaf", "grow", GCOL, None),
        P(None, GCOL, None),
        P(None, GCOL, None),
        P(None, GCOL, None),
    )
    out_specs = (
        P("leaf", "grow", GCOL, None, None),
        P("leaf", "grow", GCOL, None),
        P(None, GCOL, None),
    )
    return jax.shard_map(local, mesh=split, in_specs=in_specs, out_specs=out_specs, check_vma=False)
```

```python
import jax
import jax.numpy as jnp
from jax import lax
from jax.experimental import pallas as pl
from jax.experimental.pallas import tpu as pltpu
from jax.sharding import Mesh
from jax.sharding import PartitionSpec as P

GX, GC = "gcol_0", "gcol_1"
GCOL = (GX, GC)
LG = ("leaf", "grow")
PRECISE = lax.Precision.HIGHEST


def dot(a, b, ca, cb):
    return lax.dot_general(
        a, b, (((ca,), (cb,)), ((), ())), precision=PRECISE, preferred_element_type=jnp.float32
    )


def swap(x, axis):
    return lax.all_to_all(x, axis, split_axis=0, concat_axis=0, tiled=True)


def shift(x, axis, step):
    n = lax.axis_size(axis)
    return lax.ppermute(x, axis, [(s, (s + step) % n) for s in range(n)])


def f32(*shape):
    return jax.ShapeDtypeStruct(shape, jnp.float32)


def kernel_call(body, outs, *args, scalars=0, scratch=(), limit=24):
    specs = [pl.BlockSpec(memory_space=pltpu.SMEM)] * scalars
    specs += [pl.BlockSpec(memory_space=pltpu.VMEM)] * (len(args) - scalars)
    out_specs = jax.tree.map(lambda _: pl.BlockSpec(memory_space=pltpu.VMEM), outs)
    return pl.pallas_call(
        body, out_shape=outs, in_specs=specs, out_specs=out_specs, scratch_shapes=scratch,
        compiler_params=pltpu.CompilerParams(vmem_limit_bytes=limit and limit << 20),
    )(*args)


def split(x):
    high = x.astype(jnp.bfloat16)
    return high, (x - high.astype(jnp.float32)).astype(jnp.bfloat16)


def dot3(a, b, ca, cb):
    def one(x, y):
        return lax.dot_general(
            x, y, (((ca,), (cb,)), ((), ())), preferred_element_type=jnp.float32
        )

    (ah, al), (bh, bl) = a, b
    return one(ah, bh) + (one(ah, bl) + one(al, bh))


def pack_kernel(im, um, it, ut, w, t, sems):
    share = im.shape[0]
    copies = [
        pltpu.make_async_copy(src, out.at[pl.ds(at * share, src.shape[0])], sems.at[i])
        for i, (src, out, at) in enumerate([(im, w, 0), (um, w, 1), (it, t, 0), (ut, t, 2)])
    ]
    for c in copies:
        c.start()
    for c in copies:
        c.wait()


def leaf_kernel(me, present, il, ll, rl, rm, rt, lead_in, sent):
    n_g, cols, _ = sent.shape
    block = il.shape[0]
    share = block // n_g
    kept = present[0].astype(jnp.float32)
    fwd = dot3(split(rl[...].T), split(il[...]), 1, 1)
    lead_in[...] = fwd
    part = dot3(split(fwd), split(ll[...]), 1, 1) * kept
    lane = lax.broadcasted_iota(jnp.int32, (1, block), 1)
    own = (lane >= me[0] * share) & (lane < (me[0] + 1) * share)
    part = jnp.where(own, jnp.concatenate([rm[...].T] * n_g, axis=1), 0.0) - part
    tops = jnp.concatenate([rt[0].T, rt[1].T], axis=1)
    for d in range(n_g):
        sent[d, :, :block] = part[d * cols : (d + 1) * cols]
        sent[d, :, block:] = tops[d * cols : (d + 1) * cols]


def fill(high, low, blocks, part, share):
    n = 0
    for ref in blocks:
        for s in range(ref.shape[0] // (3 * share)):
            at = (3 * s + part) * share
            h, l = split(ref[at : at + share])
            high[n * share : (n + 1) * share] = h
            low[n * share : (n + 1) * share] = l
            n += 1
    return high[...], low[...]


def mid_kernel(got, mine, other, pieces, mf_out, high, low):
    blocks = [mine, other]
    n_g, cols, _ = got.shape
    block = other.shape[1]
    share = block // n_g
    rhs = got[0, :, :block]
    for c in range(1, n_g):
        rhs = rhs + got[c, :, :block]
    mf = dot3(split(rhs), fill(high.at[0], low.at[0], blocks, 0, share), 1, 1)
    mf_out[...] = mf
    mfs = split(mf)
    rows = pieces.shape[1]
    per = cols // rows
    for k in range(2):
        tp = dot3(mfs, fill(high.at[1 + k], low.at[1 + k], blocks, 1 + k, share), 1, 0)
        for j in range(block // 128):
            for i in range(per):
                at = (k * (block // 128) + j) * per + i
                pieces[at] = tp[i * rows : (i + 1) * rows, j * 128 : (j + 1) * 128]


def sum_kernel(pieces, out):
    total = jnp.sum(pieces[...], axis=0)
    out[...] = jnp.broadcast_to(total[None], out.shape)


def top_kernel(got, total, mf, t0, t1, t2, t3, mine, other, back, r, high, low, w_high, w_low):
    n_g, cols, _ = got.shape
    block = other.shape[1]
    share = block // n_g
    rows = total.shape[1]
    per = cols // rows
    for j in range(2 * block // 128):
        for i in range(per):
            r[i * rows : (i + 1) * rows, j * 128 : (j + 1) * 128] = total[j * per + i]
    for k in range(2):
        rt = jnp.concatenate(
            [got[c, :, block + k * share : block + (k + 1) * share] for c in range(n_g)], axis=1
        )
        r[:, k * block : (k + 1) * block] = rt - r[:, k * block : (k + 1) * block]
    it0, it1, ut = (
        fill(high.at[p], low.at[p], [t0, t1, t2, t3], p, share) for p in range(3)
    )
    f0 = dot3(split(r[:, :block]), it0, 1, 1)
    f1 = dot3(split(r[:, block:] - dot3(split(f0), ut, 1, 0)), it1, 1, 1)
    s1 = dot3(split(f1), it1, 1, 0)
    s1s = split(s1)
    s0 = dot3(split(f0 - dot3(s1s, ut, 1, 1)), it0, 1, 0)
    im, um0, um1 = (fill(w_high.at[p], w_low.at[p], [mine, other], p, share) for p in range(3))
    mr = mf[...] - dot3(split(s0), um0, 1, 1) - dot3(s1s, um1, 1, 1)
    sm = dot3(split(mr), im, 1, 0)
    for d in range(n_g):
        back[d, :, :block] = sm
        back[d, :, block : block + share] = s0[:, d * share : (d + 1) * share]
        back[d, :, block + share :] = s1[:, d * share : (d + 1) * share]


def end_kernel(me, back, link, lead, leaf_out, mid_out, top_out):
    n_g, cols, _ = back.shape
    block = link.shape[0]
    share = block // n_g
    both = back[...].reshape(n_g * cols, back.shape[2])
    sm = both[:, :block]
    leaf_out[...] = lead[...] - dot3(split(link[...]), split(sm), 1, 1)
    mine = jnp.zeros((n_g * cols, share), jnp.float32)
    for c in range(n_g):
        mine = jnp.where(me[0] == c, sm[:, c * share : (c + 1) * share], mine)
    mid_out[...] = mine.T
    for k in range(2):
        top_out[k] = both[:, block + k * share : block + (k + 1) * share].T


def local(
    right_leaf,
    inverse_leaf,
    lower_leaf,
    present,
    right_middle,
    inverse_middle,
    upper_middle,
    right_top,
    inverse_top,
    upper_top,
):
    n_lg = lax.axis_size(LG)
    n_g = lax.axis_size(GCOL)
    block, nrhs = right_leaf.shape[-2:]
    share = block // n_g
    cols = nrhs // n_g
    me = lax.axis_index(GCOL)
    il, ll, rl = inverse_leaf[0, 0, 0], lower_leaf[0, 0, 0], right_leaf[0, 0, 0]
    kept = present[0, 0, 0].astype(jnp.float32)

    any_spec = pl.BlockSpec(memory_space=pl.ANY)
    vmem_spec = pl.BlockSpec(memory_space=pltpu.VMEM)
    w, t = pl.pallas_call(
        pack_kernel,
        out_shape=(f32(3 * share, block), f32(3 * share, block)),
        in_specs=[any_spec] * 4,
        out_specs=(vmem_spec, vmem_spec),
        scratch_shapes=[pltpu.SemaphoreType.DMA((4,))],
        name="pack",
    )(
        inverse_middle[0, 0],
        upper_middle.reshape(2 * share, block),
        inverse_top.reshape(2 * share, block),
        upper_top[0],
    )
    ws = [w, shift(w, GX, 1), shift(w, GX, -1), shift(w, GX, 2)]
    t = jnp.concatenate([t, shift(t, GC, 1)], axis=0)
    leaf_fwd, sent = kernel_call(
        leaf_kernel,
        (f32(nrhs, block), f32(n_g, cols, block + 2 * share)),
        me.reshape(1).astype(jnp.int32), present.reshape(1), il, ll, rl, right_middle[0, 0], right_top,
        scalars=2, limit=None,
    )
    lead = dot(il, leaf_fwd, 0, 1)
    link = dot(il, ll, 0, 1) * kept
    got = swap(sent, GCOL)
    mine = jnp.concatenate(ws, axis=0)
    other = shift(mine, GC, 1)
    t2 = shift(t, GX, 2)
    t1, t3 = shift(t, GX, 1), shift(t, GX, -1)
    halves = pltpu.VMEM((3, block, block), jnp.bfloat16)
    pieces, mf = kernel_call(
        mid_kernel,
        (f32(n_lg, 2 * cols * block // 128 // n_lg, 128), f32(cols, block)),
        got, mine, other, scratch=[halves, halves],
    )
    arrived = swap(pieces, LG)
    total = kernel_call(sum_kernel, pieces, arrived)
    total = swap(total, LG)
    back = kernel_call(
        top_kernel, f32(n_g, cols, block + 2 * share), got, total, mf, t, t1, t2, t3, mine, other,
        scratch=[pltpu.VMEM((cols, 2 * block), jnp.float32), halves, halves, halves, halves],
    )
    back = swap(back, GCOL)
    leaf_back, solve_middle, solve_top = kernel_call(
        end_kernel,
        (f32(block, nrhs), f32(share, nrhs), f32(2, share, nrhs)),
        me.reshape(1).astype(jnp.int32), back, link, lead, scalars=1,
    )
    return (leaf_back[None, None, None], solve_middle[None, None], solve_top)


def solution(mesh):
    split = Mesh(
        mesh.devices.reshape(mesh.shape["leaf"], mesh.shape["grow"], mesh.shape["gcol"] // 2, 2),
        ("leaf", "grow", GX, GC),
    )
    in_specs = (
        P("leaf", "grow", GCOL, None, None),
        P("leaf", "grow", GCOL, None, None),
        P("leaf", "grow", GCOL, None, None),
        P("leaf", "grow", GCOL),
        P("leaf", "grow", GCOL, None),
        P("leaf", "grow", GCOL, None),
        P(None, "leaf", "grow", GCOL, None),
        P(None, GCOL, None),
        P(None, GCOL, None),
        P(None, GCOL, None),
    )
    out_specs = (
        P("leaf", "grow", GCOL, None, None),
        P("leaf", "grow", GCOL, None),
        P(None, GCOL, None),
    )
    return jax.shard_map(local, mesh=split, in_specs=in_specs, out_specs=out_specs, check_vma=False)
```

```python
import jax
import jax.numpy as jnp
from jax import lax
from jax.experimental import pallas as pl
from jax.experimental.pallas import tpu as pltpu
from jax.sharding import Mesh
from jax.sharding import PartitionSpec as P

GX, GC = "gcol_0", "gcol_1"
GCOL = (GX, GC)
LG = ("leaf", "grow")
PRECISE = lax.Precision.HIGHEST


def dot(a, b, ca, cb):
    return lax.dot_general(
        a, b, (((ca,), (cb,)), ((), ())), precision=PRECISE, preferred_element_type=jnp.float32
    )


def swap(x, axis):
    return lax.all_to_all(x, axis, split_axis=0, concat_axis=0, tiled=True)


def shift(x, axis, step):
    n = lax.axis_size(axis)
    return lax.ppermute(x, axis, [(s, (s + step) % n) for s in range(n)])


def f32(*shape):
    return jax.ShapeDtypeStruct(shape, jnp.float32)


def kernel_call(body, outs, *args, scalars=0, scratch=(), limit=24):
    specs = [pl.BlockSpec(memory_space=pltpu.SMEM)] * scalars
    specs += [pl.BlockSpec(memory_space=pltpu.VMEM)] * (len(args) - scalars)
    out_specs = jax.tree.map(lambda _: pl.BlockSpec(memory_space=pltpu.VMEM), outs)
    return pl.pallas_call(
        body, out_shape=outs, in_specs=specs, out_specs=out_specs, scratch_shapes=scratch,
        compiler_params=pltpu.CompilerParams(vmem_limit_bytes=limit and limit << 20),
    )(*args)


def split(x):
    high = x.astype(jnp.bfloat16)
    return high, (x - high.astype(jnp.float32)).astype(jnp.bfloat16)


def dot3(a, b, ca, cb):
    def one(x, y):
        return lax.dot_general(
            x, y, (((ca,), (cb,)), ((), ())), preferred_element_type=jnp.float32
        )

    (ah, al), (bh, bl) = a, b
    m = ah.shape[0]
    if ca == 1 and m < 128:
        both = one(jnp.concatenate([ah, al], axis=0), bh)
        return both[:m] + (one(ah, bl) + both[m:])
    return one(ah, bh) + (one(ah, bl) + one(al, bh))


def pack_kernel(im, um, it, ut, w, t, sems):
    share = im.shape[0]
    copies = [
        pltpu.make_async_copy(src, out.at[pl.ds(at * share, src.shape[0])], sems.at[i])
        for i, (src, out, at) in enumerate([(im, w, 0), (um, w, 1), (it, t, 0), (ut, t, 2)])
    ]
    for c in copies:
        c.start()
    for c in copies:
        c.wait()


def leaf_kernel(me, present, il, ll, rl, rm, rt, lead_in, sent):
    n_g, cols, _ = sent.shape
    block = il.shape[0]
    share = block // n_g
    kept = present[0].astype(jnp.float32)
    fwd = dot3(split(rl[...].T), split(il[...]), 1, 1)
    lead_in[...] = fwd
    part = dot3(split(fwd), split(ll[...]), 1, 1) * kept
    lane = lax.broadcasted_iota(jnp.int32, (1, block), 1)
    own = (lane >= me[0] * share) & (lane < (me[0] + 1) * share)
    part = jnp.where(own, jnp.concatenate([rm[...].T] * n_g, axis=1), 0.0) - part
    tops = jnp.concatenate([rt[0].T, rt[1].T], axis=1)
    for d in range(n_g):
        sent[d, :, :block] = part[d * cols : (d + 1) * cols]
        sent[d, :, block:] = tops[d * cols : (d + 1) * cols]


def fill(high, low, blocks, part, share):
    n = 0
    for ref in blocks:
        for s in range(ref.shape[0] // (3 * share)):
            at = (3 * s + part) * share
            h, l = split(ref[at : at + share])
            high[n * share : (n + 1) * share] = h
            low[n * share : (n + 1) * share] = l
            n += 1
    return high[...], low[...]


def mid_kernel(got, mine, other, pieces, mf_out, high, low):
    blocks = [mine, other]
    n_g, cols, _ = got.shape
    block = other.shape[1]
    share = block // n_g
    rhs = got[0, :, :block]
    for c in range(1, n_g):
        rhs = rhs + got[c, :, :block]
    mf = dot3(split(rhs), fill(high.at[0], low.at[0], blocks, 0, share), 1, 1)
    mf_out[...] = mf
    mfs = split(mf)
    rows = pieces.shape[1]
    per = cols // rows
    for k in range(2):
        tp = dot3(mfs, fill(high.at[1 + k], low.at[1 + k], blocks, 1 + k, share), 1, 0)
        for j in range(block // 128):
            for i in range(per):
                at = (k * (block // 128) + j) * per + i
                pieces[at] = tp[i * rows : (i + 1) * rows, j * 128 : (j + 1) * 128]


def sum_kernel(pieces, out):
    total = jnp.sum(pieces[...], axis=0)
    out[...] = jnp.broadcast_to(total[None], out.shape)


def top_kernel(late, got, total, mf, t0, t1, t2, t3, mine, other, back, r, high, low, w_high, w_low):
    n_g, cols, _ = got.shape
    block = other.shape[1]
    share = block // n_g
    rows = total.shape[1]
    per = cols // rows
    for j in range(2 * block // 128):
        for i in range(per):
            r[i * rows : (i + 1) * rows, j * 128 : (j + 1) * 128] = total[j * per + i]
    for k in range(2):
        rt = jnp.concatenate(
            [got[c, :, block + k * share : block + (k + 1) * share] for c in range(n_g)], axis=1
        )
        r[:, k * block : (k + 1) * block] = rt - r[:, k * block : (k + 1) * block]
    it0, it1, ut = (
        fill(high.at[p], low.at[p], [t0, t1, t2, t3], p, share) for p in range(3)
    )
    f0 = dot3(split(r[:, :block]), it0, 1, 1)
    f1 = dot3(split(r[:, block:] - dot3(split(f0), ut, 1, 0)), it1, 1, 1)
    s1 = dot3(split(f1), it1, 1, 0)
    s1s = split(s1)
    s0 = dot3(split(f0 - dot3(s1s, ut, 1, 1)), it0, 1, 0)
    im, um0, um1 = (fill(w_high.at[p], w_low.at[p], [mine, other], p, share) for p in range(3))
    mr = mf[...] - dot3(split(s0), um0, 1, 1) - dot3(s1s, um1, 1, 1)
    sm = dot3(split(mr), im, 1, 0)
    for d in range(n_g):
        back[d, :, :block] = sm
        back[d, :, block : block + share] = s0[:, d * share : (d + 1) * share]
        back[d, :, block + share :] = s1[:, d * share : (d + 1) * share]


def end_kernel(me, present, back, link, lead, leaf_out, mid_out, top_out):
    n_g, cols, _ = back.shape
    block = link.shape[0]
    share = block // n_g
    both = back[...].reshape(n_g * cols, back.shape[2])
    sm = both[:, :block]
    kept = present[0].astype(jnp.float32)
    leaf_out[...] = lead[...] - kept * dot3(split(link[...]), split(sm), 1, 1)
    mine = jnp.zeros((n_g * cols, share), jnp.float32)
    for c in range(n_g):
        mine = jnp.where(me[0] == c, sm[:, c * share : (c + 1) * share], mine)
    mid_out[...] = mine.T
    for k in range(2):
        top_out[k] = both[:, block + k * share : block + (k + 1) * share].T


def local(
    right_leaf,
    inverse_leaf,
    lower_leaf,
    present,
    right_middle,
    inverse_middle,
    upper_middle,
    right_top,
    inverse_top,
    upper_top,
):
    n_lg = lax.axis_size(LG)
    n_g = lax.axis_size(GCOL)
    block, nrhs = right_leaf.shape[-2:]
    share = block // n_g
    cols = nrhs // n_g
    me = lax.axis_index(GCOL)
    il, ll, rl = inverse_leaf[0, 0, 0], lower_leaf[0, 0, 0], right_leaf[0, 0, 0]

    any_spec = pl.BlockSpec(memory_space=pl.ANY)
    vmem_spec = pl.BlockSpec(memory_space=pltpu.VMEM)
    w, t = pl.pallas_call(
        pack_kernel,
        out_shape=(f32(3 * share, block), f32(3 * share, block)),
        in_specs=[any_spec] * 4,
        out_specs=(vmem_spec, vmem_spec),
        scratch_shapes=[pltpu.SemaphoreType.DMA((4,))],
        name="pack",
    )(inverse_middle[0, 0], upper_middle.reshape(2 * share, block), inverse_top.reshape(2 * share, block), upper_top[0])
    ws = [w, shift(w, GX, 1), shift(w, GX, -1), shift(w, GX, 2)]
    t = jnp.concatenate([t, shift(t, GC, 1)], axis=0)
    leaf_fwd, sent = kernel_call(
        leaf_kernel,
        (f32(nrhs, block), f32(n_g, cols, block + 2 * share)),
        me.reshape(1).astype(jnp.int32), present.reshape(1), il, ll, rl, right_middle[0, 0], right_top,
        scalars=2, limit=None,
    )
    lead = dot(il, leaf_fwd, 0, 1)
    link = dot(il, ll, 0, 1)
    got = swap(sent, GCOL)
    mine = jnp.concatenate(ws, axis=0)
    other = shift(mine, GC, 1)
    t2 = shift(t, GX, 2)
    t1, t3 = shift(t, GX, 1), shift(t, GX, -1)
    halves = pltpu.VMEM((3, block, block), jnp.bfloat16)
    pieces, mf = kernel_call(
        mid_kernel,
        (f32(n_lg, 2 * cols * block // 128 // n_lg, 128), f32(cols, block)),
        got, mine, other, scratch=[halves, halves],
    )
    arrived = swap(pieces, LG)
    total = kernel_call(sum_kernel, pieces, arrived)
    total = swap(total, LG)
    late = lax.slice(total, (0, 0, 0), (1, 1, 128))
    back = kernel_call(
        top_kernel, f32(n_g, cols, block + 2 * share), late, got, total, mf, t, t1, t2, t3, mine, other,
        scratch=[pltpu.VMEM((cols, 2 * block), jnp.float32), halves, halves, halves, halves],
    )
    back = swap(back, GCOL)
    leaf_back, solve_middle, solve_top = kernel_call(
        end_kernel,
        (f32(block, nrhs), f32(share, nrhs), f32(2, share, nrhs)),
        me.reshape(1).astype(jnp.int32), present.reshape(1), back, link, lead, scalars=2,
    )
    return (leaf_back[None, None, None], solve_middle[None, None], solve_top)


def solution(mesh):
    split = Mesh(
        mesh.devices.reshape(mesh.shape["leaf"], mesh.shape["grow"], mesh.shape["gcol"] // 2, 2),
        ("leaf", "grow", GX, GC),
    )
    in_specs = (
        P("leaf", "grow", GCOL, None, None),
        P("leaf", "grow", GCOL, None, None),
        P("leaf", "grow", GCOL, None, None),
        P("leaf", "grow", GCOL),
        P("leaf", "grow", GCOL, None),
        P("leaf", "grow", GCOL, None),
        P(None, "leaf", "grow", GCOL, None),
        P(None, GCOL, None),
        P(None, GCOL, None),
        P(None, GCOL, None),
    )
    out_specs = (
        P("leaf", "grow", GCOL, None, None),
        P("leaf", "grow", GCOL, None),
        P(None, GCOL, None),
    )
    return jax.shard_map(local, mesh=split, in_specs=in_specs, out_specs=out_specs, check_vma=False)
```

```python
import jax
import jax.numpy as jnp
from jax import lax
from jax.experimental import pallas as pl
from jax.experimental.pallas import tpu as pltpu
from jax.sharding import Mesh
from jax.sharding import PartitionSpec as P

GX, GC = "gcol_0", "gcol_1"
GCOL = (GX, GC)
LG = ("leaf", "grow")
PRECISE = lax.Precision.HIGHEST


def dot(a, b, ca, cb):
    return lax.dot_general(
        a, b, (((ca,), (cb,)), ((), ())), precision=PRECISE, preferred_element_type=jnp.float32
    )


def swap(x, axis):
    return lax.all_to_all(x, axis, split_axis=0, concat_axis=0, tiled=True)


def shift(x, axis, step):
    n = lax.axis_size(axis)
    return lax.ppermute(x, axis, [(s, (s + step) % n) for s in range(n)])


def f32(*shape):
    return jax.ShapeDtypeStruct(shape, jnp.float32)


def kernel_call(body, outs, *args, scalars=0, scratch=(), limit=24, space=pltpu.VMEM):
    specs = [pl.BlockSpec(memory_space=pltpu.SMEM)] * scalars
    specs += [pl.BlockSpec(memory_space=space)] * (len(args) - scalars)
    out_specs = jax.tree.map(lambda _: pl.BlockSpec(memory_space=pltpu.VMEM), outs)
    return pl.pallas_call(
        body, out_shape=outs, in_specs=specs, out_specs=out_specs, scratch_shapes=scratch,
        compiler_params=pltpu.CompilerParams(vmem_limit_bytes=limit and limit << 20),
    )(*args)


def split(x):
    high = x.astype(jnp.bfloat16)
    return high, (x - high.astype(jnp.float32)).astype(jnp.bfloat16)


def dot3(a, b, ca, cb):
    def one(x, y):
        return lax.dot_general(
            x, y, (((ca,), (cb,)), ((), ())), preferred_element_type=jnp.float32
        )

    (ah, al), (bh, bl) = a, b
    m = ah.shape[0]
    if ca == 1 and m < 128:
        both = one(jnp.concatenate([ah, al], axis=0), bh)
        return both[:m] + (one(ah, bl) + both[m:])
    return one(ah, bh) + (one(ah, bl) + one(al, bh))


def pack_kernel(im, um, it, ut, w, t, sems):
    share = im.shape[0]
    copies = [
        pltpu.make_async_copy(src, out.at[pl.ds(at * share, src.shape[0])], sems.at[i])
        for i, (src, out, at) in enumerate([(im, w, 0), (um, w, 1), (it, t, 0), (ut, t, 2)])
    ]
    for c in copies:
        c.start()
    for c in copies:
        c.wait()


def leaf_kernel(me, present, il_far, ll_far, rl_far, rm_far, rt_far, lead_in, sent, il, ll, rl, rm, rt, sems):
    pairs = [(rl_far, rl), (il_far, il), (ll_far, ll), (rm_far, rm), (rt_far, rt)]
    copies = [pltpu.make_async_copy(a, b, sems.at[i]) for i, (a, b) in enumerate(pairs)]
    for c in copies:
        c.start()
    n_g, cols, _ = sent.shape
    block = il.shape[0]
    share = block // n_g
    kept = present[0].astype(jnp.float32)
    copies[0].wait()
    copies[1].wait()
    fwd = dot3(split(rl[...].T), split(il[...]), 1, 1)
    lead_in[...] = fwd
    for c in copies[2:]:
        c.wait()
    part = dot3(split(fwd), split(ll[...]), 1, 1) * kept
    lane = lax.broadcasted_iota(jnp.int32, (1, block), 1)
    own = (lane >= me[0] * share) & (lane < (me[0] + 1) * share)
    part = jnp.where(own, jnp.concatenate([rm[...].T] * n_g, axis=1), 0.0) - part
    tops = jnp.concatenate([rt[0].T, rt[1].T], axis=1)
    for d in range(n_g):
        sent[d, :, :block] = part[d * cols : (d + 1) * cols]
        sent[d, :, block:] = tops[d * cols : (d + 1) * cols]


def fill(high, low, blocks, part, share):
    n = 0
    for ref in blocks:
        for s in range(ref.shape[0] // (3 * share)):
            at = (3 * s + part) * share
            h, l = split(ref[at : at + share])
            high[n * share : (n + 1) * share] = h
            low[n * share : (n + 1) * share] = l
            n += 1
    return high[...], low[...]


def mid_kernel(got, mine, other, pieces, mf_out, high, low):
    blocks = [mine, other]
    n_g, cols, _ = got.shape
    block = other.shape[1]
    share = block // n_g
    rhs = got[0, :, :block]
    for c in range(1, n_g):
        rhs = rhs + got[c, :, :block]
    mf = dot3(split(rhs), fill(high.at[0], low.at[0], blocks, 0, share), 1, 1)
    mf_out[...] = mf
    mfs = split(mf)
    rows = pieces.shape[1]
    per = cols // rows
    for k in range(2):
        tp = dot3(mfs, fill(high.at[1 + k], low.at[1 + k], blocks, 1 + k, share), 1, 0)
        for j in range(block // 128):
            for i in range(per):
                at = (k * (block // 128) + j) * per + i
                pieces[at] = tp[i * rows : (i + 1) * rows, j * 128 : (j + 1) * 128]


def sum_kernel(pieces, out):
    total = jnp.sum(pieces[...], axis=0)
    out[...] = jnp.broadcast_to(total[None], out.shape)


def top_kernel(late, got, total, mf, t0, t1, t2, t3, mine, other, back, r, high, low, w_high, w_low):
    n_g, cols, _ = got.shape
    block = other.shape[1]
    share = block // n_g
    rows = total.shape[1]
    per = cols // rows
    for j in range(2 * block // 128):
        for i in range(per):
            r[i * rows : (i + 1) * rows, j * 128 : (j + 1) * 128] = total[j * per + i]
    for k in range(2):
        rt = jnp.concatenate(
            [got[c, :, block + k * share : block + (k + 1) * share] for c in range(n_g)], axis=1
        )
        r[:, k * block : (k + 1) * block] = rt - r[:, k * block : (k + 1) * block]
    it0, it1, ut = (
        fill(high.at[p], low.at[p], [t0, t1, t2, t3], p, share) for p in range(3)
    )
    f0 = dot3(split(r[:, :block]), it0, 1, 1)
    f1 = dot3(split(r[:, block:] - dot3(split(f0), ut, 1, 0)), it1, 1, 1)
    s1 = dot3(split(f1), it1, 1, 0)
    s1s = split(s1)
    s0 = dot3(split(f0 - dot3(s1s, ut, 1, 1)), it0, 1, 0)
    im, um0, um1 = (fill(w_high.at[p], w_low.at[p], [mine, other], p, share) for p in range(3))
    mr = mf[...] - dot3(split(s0), um0, 1, 1) - dot3(s1s, um1, 1, 1)
    sm = dot3(split(mr), im, 1, 0)
    for d in range(n_g):
        back[d, :, :block] = sm
        back[d, :, block : block + share] = s0[:, d * share : (d + 1) * share]
        back[d, :, block + share :] = s1[:, d * share : (d + 1) * share]


def end_kernel(me, present, back, link, lead, leaf_out, mid_out, top_out):
    n_g, cols, _ = back.shape
    block = link.shape[0]
    share = block // n_g
    both = back[...].reshape(n_g * cols, back.shape[2])
    sm = both[:, :block]
    kept = present[0].astype(jnp.float32)
    leaf_out[...] = lead[...] - kept * dot3(split(link[...]), split(sm), 1, 1)
    mine = jnp.zeros((n_g * cols, share), jnp.float32)
    for c in range(n_g):
        mine = jnp.where(me[0] == c, sm[:, c * share : (c + 1) * share], mine)
    mid_out[...] = mine.T
    for k in range(2):
        top_out[k] = both[:, block + k * share : block + (k + 1) * share].T


def local(
    right_leaf,
    inverse_leaf,
    lower_leaf,
    present,
    right_middle,
    inverse_middle,
    upper_middle,
    right_top,
    inverse_top,
    upper_top,
):
    n_lg = lax.axis_size(LG)
    n_g = lax.axis_size(GCOL)
    block, nrhs = right_leaf.shape[-2:]
    share = block // n_g
    cols = nrhs // n_g
    me = lax.axis_index(GCOL)
    il, ll, rl = inverse_leaf[0, 0, 0], lower_leaf[0, 0, 0], right_leaf[0, 0, 0]

    any_spec = pl.BlockSpec(memory_space=pl.ANY)
    vmem_spec = pl.BlockSpec(memory_space=pltpu.VMEM)
    w, t = pl.pallas_call(
        pack_kernel,
        out_shape=(f32(3 * share, block), f32(3 * share, block)),
        in_specs=[any_spec] * 4,
        out_specs=(vmem_spec, vmem_spec),
        scratch_shapes=[pltpu.SemaphoreType.DMA((4,))],
        name="pack",
    )(inverse_middle[0, 0], upper_middle.reshape(2 * share, block), inverse_top.reshape(2 * share, block), upper_top[0])
    ws = [w, shift(w, GX, 1), shift(w, GX, -1), shift(w, GX, 2)]
    t = jnp.concatenate([t, shift(t, GC, 1)], axis=0)
    leaf_fwd, sent = kernel_call(
        leaf_kernel,
        (f32(nrhs, block), f32(n_g, cols, block + 2 * share)),
        me.reshape(1).astype(jnp.int32), present.reshape(1), il, ll, rl, right_middle[0, 0], right_top,
        scalars=2, limit=None, space=pl.ANY,
        scratch=[
            *(pltpu.VMEM(a.shape, jnp.float32) for a in (il, ll, rl, right_middle[0, 0], right_top)),
            pltpu.SemaphoreType.DMA((5,)),
        ],
    )
    lead = dot(il, leaf_fwd, 0, 1)
    link = dot(il, ll, 0, 1)
    got = swap(sent, GCOL)
    mine = jnp.concatenate(ws, axis=0)
    other = shift(mine, GC, 1)
    t2 = shift(t, GX, 2)
    t1, t3 = shift(t, GX, 1), shift(t, GX, -1)
    halves = pltpu.VMEM((3, block, block), jnp.bfloat16)
    pieces, mf = kernel_call(
        mid_kernel,
        (f32(n_lg, 2 * cols * block // 128 // n_lg, 128), f32(cols, block)),
        got, mine, other, scratch=[halves, halves],
    )
    arrived = swap(pieces, LG)
    total = kernel_call(sum_kernel, pieces, arrived)
    total = swap(total, LG)
    late = lax.slice(total, (0, 0, 0), (1, 1, 128))
    back = kernel_call(
        top_kernel, f32(n_g, cols, block + 2 * share), late, got, total, mf, t, t1, t2, t3, mine, other,
        scratch=[pltpu.VMEM((cols, 2 * block), jnp.float32), halves, halves, halves, halves],
    )
    back = swap(back, GCOL)
    leaf_back, solve_middle, solve_top = kernel_call(
        end_kernel,
        (f32(block, nrhs), f32(share, nrhs), f32(2, share, nrhs)),
        me.reshape(1).astype(jnp.int32), present.reshape(1), back, link, lead, scalars=2,
    )
    return (leaf_back[None, None, None], solve_middle[None, None], solve_top)


def solution(mesh):
    split = Mesh(
        mesh.devices.reshape(mesh.shape["leaf"], mesh.shape["grow"], mesh.shape["gcol"] // 2, 2),
        ("leaf", "grow", GX, GC),
    )
    in_specs = (
        P("leaf", "grow", GCOL, None, None),
        P("leaf", "grow", GCOL, None, None),
        P("leaf", "grow", GCOL, None, None),
        P("leaf", "grow", GCOL),
        P("leaf", "grow", GCOL, None),
        P("leaf", "grow", GCOL, None),
        P(None, "leaf", "grow", GCOL, None),
        P(None, GCOL, None),
        P(None, GCOL, None),
        P(None, GCOL, None),
    )
    out_specs = (
        P("leaf", "grow", GCOL, None, None),
        P("leaf", "grow", GCOL, None),
        P(None, GCOL, None),
    )
    return jax.shard_map(local, mesh=split, in_specs=in_specs, out_specs=out_specs, check_vma=False)
```
